256 devices in a mesh: ctx: 8 (over x, core), head: 32 (over y, z).
Axes of the slice: x: 4, y: 4, z: 8, core: 2. Of those that a mesh axis runs over, the one named last changes fastest.
Arguments:
- queries: bfloat16 [4096, 64, 128], P('ctx', 'head'), may hold values from -42 to 42
- cached_keys: bfloat16 [4, 32768, 128], P(None, 'ctx'), may hold values from -5 to 5
- cached_values: bfloat16 [4, 32768, 128], P(None, 'ctx'), may hold values from -6 to 6
- grad_out: bfloat16 [4096, 64, 128], P('ctx', 'head'), may hold values from -96 to 96
- chosen: int32 [4, 16, 16], P(None, 'ctx'), may hold values from 0 to 511, as said below
- counts: int32 [4, 16], P(None, 'ctx'), may hold values from 8 to 16, as said below
Outputs:
- grad_query: bfloat16 [4096, 64, 128], P('ctx', 'head')
- grad_keys: bfloat16 [4, 32768, 128], P(None, ('ctx', 'head'))
- grad_values: bfloat16 [4, 32768, 128], P(None, ('ctx', 'head'))
The draws below stay inside these ranges and needn't reach their ends.
Inputs may be any that keep to these rules, and one draw needn't show every extreme that they name: For t < counts[g, b] the entries chosen[g, b, t] are distinct; entries at t >= counts[g, b] are padding. For each group and each run of 2 query blocks starting at a multiple of 2, at most 8 live entries fall in one range of 64 blocks starting at a multiple of 64, and in every group one range receives exactly 8 from every such run. `counts`: in every group some query block has 16 live entries.
All inputs are finite; a program needn't handle non-finite values.
Results may differ from the reference program's by a relative error of at most 0.02.
Values may be sent and summed in bfloat16 or wider, within the bound.
No kernel may reach another device: no remote copies, remote signals or barrier semaphores. Data moves between devices by JAX's collectives and lax.ppermute only.
A program may use at most 64 MiB of HBM per device.

```python
import jax
import jax.numpy as jnp
from jax import lax

DH = 128
HPG = 16
KBS = 64
TOPB = 16
QBS = 256
HOT = 4
HEADS = 64
GROUPS = 4
OWNERS = 8
BLK_OWN = 64
KVTOK = 32768
QBLOCKS = 16
QTOK = 4096


def selection(key):
    flow_step = jax.random.fold_in(key, 4049)
    streams = jax.random.split(flow_step, 7)
    hot_owner = jax.random.randint(streams[0], (GROUPS, 1, 1), 0, OWNERS)
    counts = jax.random.randint(streams[1], (GROUPS, QBLOCKS), 8, TOPB + 1)
    full_block = jax.random.randint(streams[2], (GROUPS, 1), 0, QBLOCKS)
    counts = jnp.where(jnp.arange(QBLOCKS)[None, :] == full_block, TOPB, counts)
    offset_draw = jax.random.randint(streams[3], (GROUPS, QBLOCKS, 1), 0, OWNERS - 1)
    base_hot = jax.random.randint(streams[4], (GROUPS, QBLOCKS, 1), 0, BLK_OWN)
    base_other = jax.random.randint(streams[5], (GROUPS, QBLOCKS, 1), 0, BLK_OWN)
    slot_index = jnp.arange(TOPB)[None, None, :]
    rest_rank = slot_index - HOT
    owner_index = jnp.where(slot_index < HOT, hot_owner, (hot_owner + 1 + (rest_rank + offset_draw) % (OWNERS - 1)) % OWNERS)
    local_index = jnp.where(slot_index < HOT, (base_hot + slot_index) % BLK_OWN, (base_other + rest_rank) % BLK_OWN)
    padding = jax.random.randint(streams[6], (GROUPS, QBLOCKS, TOPB), 0, OWNERS * BLK_OWN)
    chosen = jnp.where(slot_index < counts[:, :, None], owner_index * BLK_OWN + local_index, padding)
    return (chosen.astype(jnp.int32), counts.astype(jnp.int32))


def draw_chosen(key, part):
    return selection(key)[0]


def draw_counts(key, part):
    return selection(key)[1]


def draw_cached_keys(key, part):
    flow_step = jax.random.fold_in(key, 811)
    sample = jnp.clip(jax.random.normal(flow_step, (GROUPS, KVTOK, DH), jnp.float32), -5.0, 5.0)
    return sample.astype(jnp.bfloat16)


def draw_queries(key, part):
    flow_step = jax.random.fold_in(key, 977)
    sample = jnp.clip(jax.random.normal(flow_step, (QTOK, HEADS, DH), jnp.float32), -6.0, 6.0)
    return sample.astype(jnp.bfloat16)


def block_levels(key, dims, cuts, least, high):
    def one(position, parts):
        steps = jax.random.uniform(jax.random.fold_in(jax.random.fold_in(key, 6), position), (parts,), jnp.float32, least / len(cuts), high / len(cuts))
        return jnp.repeat(jnp.exp(steps), dims[position] // parts).reshape((-1,) + (1,) * (len(dims) - position - 1))

    level = one(*cuts[0])
    for cut in cuts[1:]:
        level = level * one(*cut)
    return level


def noise(key, shape, width, most, pieces=(), dtype=jnp.bfloat16):
    array = width * jax.random.normal(key, shape, jnp.float32)
    if pieces:
        array = array * block_levels(key, shape, pieces, -0.22, 0.18)
    return jnp.clip(array, -most, most).astype(dtype)


def setup_inputs(seed: int = 0) -> dict:
    splits = jax.random.split(jax.random.key(seed), 7)
    return {
        "queries": draw_queries(jax.random.fold_in(splits[6], 71), 0),
        "cached_keys": draw_cached_keys(jax.random.fold_in(splits[6], 71), 0),
        "cached_values": noise(splits[2], (GROUPS, KVTOK, DH), 1.0, 6.0, ((1, 8),)),
        "grad_out": noise(splits[3], (QTOK, HEADS, DH), 16.0, 96.0, ((0, 8), (1, 32))),
        "chosen": draw_chosen(jax.random.fold_in(splits[6], 71), 0),
        "counts": draw_counts(jax.random.fold_in(splits[6], 71), 0),
    }


def group_pass(queries_g, grad_g, keys_g, values_g, chosen_g, counts_g):
    inv_root = DH ** -0.5
    query_all = queries_g.reshape(QBLOCKS, QBS, HPG, DH)
    grad_all = grad_g.reshape(QBLOCKS, QBS, HPG, DH)

    def visit(totals, inputs):
        grad_k, grad_v = totals
        query_block, grad_block, picked, live_count = inputs
        token_index = (picked[:, None] * KBS + jnp.arange(KBS)[None, :]).reshape(-1).astype(jnp.int32)
        key_rows = keys_g[token_index].astype(jnp.float32)
        value_rows = values_g[token_index].astype(jnp.float32)
        key_live = jnp.repeat(jnp.arange(TOPB) < live_count, KBS)
        live_mask = key_live[None, None, :]
        query_wide = query_block.astype(jnp.float32)
        grad_wide = grad_block.astype(jnp.float32)
        logit_scores = jnp.einsum("qhd,kd->hqk", query_wide, key_rows) * inv_root
        row_peak = jnp.max(jnp.where(live_mask, logit_scores, -jnp.inf), axis=-1, keepdims=True)
        weights_raw = jnp.where(live_mask, jnp.exp(logit_scores - row_peak), 0.0)
        weights = weights_raw / jnp.sum(weights_raw, axis=-1, keepdims=True)
        weight_halves = lax.optimization_barrier(weights.astype(jnp.bfloat16)).astype(jnp.float32)
        attn_out = jnp.einsum("hqk,kd->qhd", weight_halves, value_rows).astype(jnp.bfloat16)
        attn_wide = lax.optimization_barrier(attn_out).astype(jnp.float32)
        row_dot = jnp.transpose(jnp.sum(grad_wide * attn_wide, axis=-1))[:, :, None]
        grad_weights = jnp.einsum("qhd,kd->hqk", grad_wide, value_rows)
        score_gradients = (weights * (grad_weights - row_dot) * inv_root).astype(jnp.bfloat16)
        score_gradients = lax.optimization_barrier(score_gradients).astype(jnp.float32)
        grad_q = jnp.einsum("hqk,kd->qhd", score_gradients, key_rows).astype(jnp.bfloat16)
        slot_dk = jnp.einsum("hqk,qhd->kd", score_gradients, query_wide)
        slot_dv = jnp.einsum("hqk,qhd->kd", weight_halves, grad_wide)
        grad_k = grad_k.at[token_index].add(slot_dk)
        grad_v = grad_v.at[token_index].add(slot_dv)
        return (grad_k, grad_v), grad_q

    empty = jnp.zeros((KVTOK, DH), jnp.float32)
    (grad_k, grad_v), grad_q = lax.scan(visit, (empty, empty), (query_all, grad_all, chosen_g, counts_g))
    return grad_k, grad_v, grad_q.reshape(QTOK, HPG, DH)


def reference(queries, cached_keys, cached_values, grad_out, chosen, counts):
    key_parts = []
    value_parts = []
    query_parts = []
    for group_index in range(GROUPS):
        lower = group_index * HPG
        upper = lower + HPG
        grad_k, grad_v, grad_q = group_pass(queries[:, lower:upper], grad_out[:, lower:upper], cached_keys[group_index], cached_values[group_index], chosen[group_index], counts[group_index])
        key_parts.append(grad_k)
        value_parts.append(grad_v)
        query_parts.append(grad_q)
    grad_query = jnp.concatenate(query_parts, axis=1)
    grad_keys = jnp.stack(key_parts).astype(jnp.bfloat16)
    grad_values = jnp.stack(value_parts).astype(jnp.bfloat16)
    return grad_query, grad_keys, grad_values
```

```python
import jax
import jax.numpy as jnp
from jax import lax
from jax.experimental import pallas as pl
from jax.experimental.pallas import tpu as pltpu
from jax.sharding import Mesh
from jax.sharding import PartitionSpec as P

DH = 128
KBS = 64
TOPB = 16
BLK_OWN = 64
CAP = 8
OWN = 8
PIECE = 16
GROUPS = 4
ROWS = 1024
TILE = 256
QKEYS = 256
INV_ROOT = DH ** (-0.5)
LOG2E = 1.4426950408889634

BF = jnp.bfloat16
F32 = jnp.float32
I32 = jnp.int32
SMEM = pltpu.MemorySpace.SMEM
VMEM = pltpu.MemorySpace.VMEM


def request_kernel(place, chosen, counts, requests, meta, fill):
    group = place[0]
    for o in range(OWN):
        fill[o] = 0
        for r in range(CAP):
            requests[o, r] = 0
    for b in range(2):
        live_count = counts[group, b]
        meta[2 * TOPB + b] = live_count

        def visit(t, carry, b=b, live_count=live_count):
            block = chosen[group, b, t]
            owner = block // BLK_OWN

            @pl.when(t < live_count)
            def _():
                rank = fill[owner]
                requests[owner, rank] = block % BLK_OWN
                fill[owner] = rank + 1
                meta[b * TOPB + t] = owner * CAP + rank

            @pl.when(t >= live_count)
            def _():
                meta[b * TOPB + t] = meta[b * TOPB]

            return carry

        lax.fori_loop(0, TOPB, visit, 0)


def gather_kernel(place, asked, keys, values, out, sem):
    group = place[0]
    first = place[2] * PIECE

    def copy_from(source):
        def visit(n, carry):
            block = asked[n // CAP, n % CAP]
            pltpu.make_async_copy(
                source.at[group, pl.ds(block * KBS + first, PIECE), :], out.at[n], sem
            ).start()
            return carry

        lax.fori_loop(0, OWN * CAP, visit, 0, unroll=8)

    @pl.when(place[1] == 0)
    def _():
        copy_from(keys)

    @pl.when(place[1] != 0)
    def _():
        copy_from(values)

    pltpu.make_async_copy(out, out, sem).wait()


def compact_kernel(meta, got, out):
    for b in range(2):

        def visit(t, carry, b=b):
            tile = got[meta[b * TOPB + t]]
            for a in range(4):
                out[2 * a + b, t] = tile
            return carry

        lax.fori_loop(0, TOPB, visit, 0, unroll=4)


def attention_kernel(meta, place, kv, query, grad, dq, dkv, kt, vt, acc, prob, half):
    step = pl.program_id(0)

    @pl.when(step == 0)
    def _():
        for n in range(4):
            cols = pl.ds(n * QKEYS, QKEYS)
            kt[:, cols] = kv[n].T
            vt[:, cols] = kv[4 + n].T
        acc[...] = jnp.zeros_like(acc)

    live_rows = meta[2 * TOPB + place[3]] * PIECE
    row = lax.broadcasted_iota(I32, (QKEYS, TILE), 0)
    live = row < live_rows
    q = query[...]
    g = grad[...]
    nt = (((1,), (1,)), ((), ()))
    peak = jnp.full((1, TILE), -jnp.inf, F32)
    for n in range(4):
        s = lax.dot_general(kv[n], q, nt, preferred_element_type=F32)
        s = jnp.where(live, s, -jnp.inf)
        prob[n] = s
        peak = jnp.maximum(peak, jnp.max(s, axis=0, keepdims=True))
    scale = INV_ROOT * LOG2E
    total = jnp.zeros((1, TILE), F32)
    for n in range(4):
        p = jnp.exp2((prob[n] - peak) * scale)
        prob[n] = p
        total = total + jnp.sum(p, axis=0, keepdims=True)
    rate = 1.0 / total
    out_t = jnp.zeros((DH, TILE), F32)
    for n in range(4):
        w = prob[n] * rate
        prob[n] = w
        wh = w.astype(BF)
        half[n] = wh
        out_t = out_t + jnp.dot(
            vt[:, n * QKEYS : (n + 1) * QKEYS], wh, preferred_element_type=F32
        )
    g_t = g.astype(F32).T
    row_dot = jnp.sum(g_t * out_t.astype(BF).astype(F32), axis=0, keepdims=True)
    dq_t = jnp.zeros((DH, TILE), F32)
    for n in range(4):
        gw = lax.dot_general(kv[4 + n], g, nt, preferred_element_type=F32)
        ds = (prob[n] * (gw - row_dot) * INV_ROOT).astype(BF)
        dq_t = dq_t + jnp.dot(
            kt[:, n * QKEYS : (n + 1) * QKEYS], ds, preferred_element_type=F32
        )
        acc[n] += jnp.dot(ds, q, preferred_element_type=F32)
        acc[4 + n] += jnp.dot(half[n], g, preferred_element_type=F32)
    dq[...] = dq_t.T.astype(BF)

    @pl.when(step == pl.num_programs(0) - 1)
    def _():
        dkv[...] = acc[...].astype(BF)


def home_kernel(meta, parts, out):
    out[...] = jnp.zeros_like(out)
    for b in range(2):

        def visit(t, carry, b=b):
            @pl.when(t < meta[2 * TOPB + b])
            def _():
                tile = parts[b, t].astype(F32)
                for a in range(1, 4):
                    tile = tile + parts[2 * a + b, t].astype(F32)
                out[meta[b * TOPB + t]] = tile.astype(BF)

            return carry

        lax.fori_loop(0, TOPB, visit, 0)


def block_kernel(asked, parts, out, acc):
    acc[...] = jnp.zeros_like(acc)

    def visit(n, carry):
        block = asked[n // CAP, n % CAP]
        acc[block] = acc[block] + parts[n].astype(F32)
        return carry

    lax.fori_loop(0, OWN * CAP, visit, 0, unroll=8)
    out[...] = acc[...].astype(BF)


def place_kernel(parts, grad_keys, grad_values):
    for g in range(GROUPS):
        for part in range(4):
            for e in range(2):
                rows = pl.ds(e * KBS + part * PIECE, PIECE)
                grad_keys[g, rows, :] = parts[g * 8 + part, e]
                grad_values[g, rows, :] = parts[g * 8 + 4 + part, e]


def shape(dims, dtype=BF):
    return jax.ShapeDtypeStruct(dims, dtype)


def whole(space=VMEM):
    return pl.BlockSpec(memory_space=space)


def call(kernel, out_shape, in_specs, out_specs, scratch=(), name=None):
    return pl.pallas_call(
        kernel,
        out_shape=out_shape,
        in_specs=in_specs,
        out_specs=out_specs,
        scratch_shapes=scratch,
        name=name,
    )


def exchange(x, axes):
    return lax.all_to_all(x, axes, split_axis=0, concat_axis=0, tiled=True)


def body(queries, cached_keys, cached_values, grad_out, chosen, counts):
    zb = lax.axis_index("zb")
    z = lax.axis_index(("za", "zb"))
    place = jnp.stack([lax.axis_index("y"), z // 4, z % 4, zb]).astype(I32)
    ring = ("za", "zb")
    query_rows = exchange(queries.reshape(ROWS, DH), "zb")
    grad_rows = exchange(grad_out.reshape(ROWS, DH), "zb")
    requests, meta = call(
        request_kernel,
        (shape((OWN, CAP), I32), shape((2 * TOPB + 2,), I32)),
        [whole(SMEM)] * 3,
        (whole(SMEM),) * 2,
        [pltpu.SMEM((OWN,), I32)],
        name="request",
    )(place, chosen, counts)
    asked = exchange(requests, "ctx")
    pieces = call(
        gather_kernel,
        shape((OWN * CAP, PIECE, DH)),
        [whole(SMEM)] * 2 + [whole(pl.ANY)] * 2,
        whole(pl.ANY),
        [pltpu.SemaphoreType.DMA],
        name="gather",
    )(place, asked, cached_keys, cached_values)
    fetched = exchange(pieces, "ctx")
    spread = call(
        compact_kernel,
        shape((8, TOPB, PIECE, DH)),
        [whole(SMEM), whole()],
        whole(),
        name="compact",
    )(meta, fetched)
    kv = exchange(spread, ring).reshape(8, QKEYS, DH)
    tiles = pl.BlockSpec((TILE, DH), lambda i: (i, 0))
    fixed = pl.BlockSpec((8, QKEYS, DH), lambda i: (0, 0, 0))
    dq_rows, slot_grads = pl.pallas_call(
        attention_kernel,
        grid=(ROWS // TILE,),
        out_shape=(shape((ROWS, DH)), shape((8, QKEYS, DH))),
        in_specs=[whole(SMEM), whole(SMEM), fixed, tiles, tiles],
        out_specs=(tiles, fixed),
        scratch_shapes=[
            pltpu.VMEM((DH, ROWS), BF),
            pltpu.VMEM((DH, ROWS), BF),
            pltpu.VMEM((8, QKEYS, DH), F32),
            pltpu.VMEM((4, QKEYS, TILE), F32),
            pltpu.VMEM((4, QKEYS, TILE), BF),
        ],
        name="attention",
    )(meta, place, kv, query_rows, grad_rows)
    grad_query = exchange(dq_rows, "zb").reshape(queries.shape)
    parts = exchange(slot_grads, ring).reshape(8, TOPB, PIECE, DH)
    home = call(
        home_kernel,
        shape((OWN * CAP, PIECE, DH)),
        [whole(SMEM), whole()],
        whole(),
        name="home",
    )(meta, parts)
    arrived = exchange(home, "ctx")
    block_sums = call(
        block_kernel,
        shape((BLK_OWN, PIECE, DH)),
        [whole(SMEM), whole()],
        whole(),
        [pltpu.VMEM((BLK_OWN, PIECE, DH), F32)],
        name="blocks",
    )(asked, arrived)
    placed = exchange(block_sums, ("y",) + ring).reshape(32, 2, PIECE, DH)
    grad_keys, grad_values = call(
        place_kernel,
        (shape((GROUPS, 2 * KBS, DH)),) * 2,
        [whole()],
        (whole(),) * 2,
        name="place",
    )(placed)
    return grad_query, grad_keys, grad_values


def solution(mesh):
    fine = Mesh(mesh.devices.reshape(8, 4, 4, 2), ("ctx", "y", "za", "zb"))
    head = ("y", "za", "zb")
    return jax.shard_map(
        body,
        mesh=fine,
        in_specs=(
            P("ctx", head, None),
            P(None, "ctx", None),
            P(None, "ctx", None),
            P("ctx", head, None),
            P(None, "ctx", None),
            P(None, "ctx"),
        ),
        out_specs=(
            P("ctx", head, None),
            P(None, ("ctx",) + head, None),
            P(None, ("ctx",) + head, None),
        ),
        check_vma=False,
    )
```
